128 devices in a mesh: row: 16 (over y, x), col: 8 (over z, core).
Axes of the slice: x: 4, y: 4, z: 4, core: 2. Of those that a mesh axis runs over, the one named last changes fastest.
Arguments:
- sample_counts: int32 [64], replicated, may hold values from 100 to 2000
- slot_silo: int32 [64], replicated, may hold values from 0 to 63, each once
- gate_weight: bfloat16 [28672, 8192], P('row', 'col'), may hold values from -3 to 3
- up_weight: bfloat16 [28672, 8192], P('row', 'col'), may hold values from -3 to 3
- down_weight: bfloat16 [8192, 28672], P('row', 'col'), may hold values from -3 to 3
- gate_a: bfloat16 [1024, 8192], P(('row', 'col')), may hold values from -6 to 6
- up_a: bfloat16 [1024, 8192], P(('row', 'col')), may hold values from -6 to 6
- down_a: bfloat16 [1024, 28672], P(('row', 'col')), may hold values from -6 to 6
- gate_b: bfloat16 [1024, 28672], P(('row', 'col')), may hold values from -6 to 6
- up_b: bfloat16 [1024, 28672], P(('row', 'col')), may hold values from -6 to 6
- down_b: bfloat16 [1024, 8192], P(('row', 'col')), may hold values from -6 to 6
Outputs:
- merged_gate: bfloat16 [28672, 8192], P('row', 'col')
- merged_up: bfloat16 [28672, 8192], P('row', 'col')
- merged_down: bfloat16 [8192, 28672], P('row', 'col')
The draws below stay inside these ranges and needn't reach their ends.
Inputs may be any that keep to these rules, and one draw needn't show every extreme that they name: `slot_silo`: a permutation of the silos.
All inputs are finite; a program needn't handle non-finite values.
Results may differ from the reference program's by a relative error of at most 0.0043.
Values may be sent and summed in bfloat16 or wider, within the bound.
A program may use at most 128 MiB of HBM per device.

```python
import jax
import jax.numpy as jnp

D = 8192
FF = 28672
RANK = 16
SILOS = 64
STACKED = 1024


def touch_ends(values, stream_key, low, top_value):
    extent = values.shape
    index_at = [jax.random.randint(jax.random.fold_in(stream_key, axis), (), 0, extent[axis]) for axis in range(len(extent))]
    values = values.at[tuple(index_at)].set(low)
    longest = extent.index(max(extent))
    index_at[longest] = (index_at[longest] + 1) % extent[longest]
    return values.at[tuple(index_at)].set(top_value)


def level_of(stream_key, extent, pieces, least, largest):
    def one(position, parts):
        heights = jax.random.uniform(jax.random.fold_in(jax.random.fold_in(stream_key, 6), position), (parts,), jnp.float32, least / len(pieces), largest / len(pieces))
        return jnp.repeat(jnp.exp(heights), extent[position] // parts).reshape((-1,) + (1,) * (len(extent) - position - 1))

    factor_of = one(*pieces[0])
    for cut in pieces[1:]:
        factor_of = factor_of * one(*cut)
    return factor_of


def gaussian(rng, shape, spread, bound, split=(), kind=jnp.bfloat16):
    array = spread * jax.random.normal(rng, shape, jnp.float32)
    if split:
        array = array * level_of(rng, shape, split, -0.22, 0.18)
    return jnp.clip(array, -bound, bound).astype(kind)


def setup_inputs(seed: int = 0) -> dict:
    seeds = jax.random.split(jax.random.key(seed), 12)
    return {
        "sample_counts": touch_ends(jax.random.randint(seeds[0], (SILOS,), 100, 2001), jax.random.fold_in(seeds[0], 1), 100, 2000).astype(jnp.int32),
        "slot_silo": jax.random.permutation(seeds[1], SILOS).astype(jnp.int32),
        "gate_weight": gaussian(seeds[2], (FF, D), 0.5, 3.0, ((0, 16), (1, 8))),
        "up_weight": gaussian(seeds[3], (FF, D), 0.5, 3.0, ((0, 16), (1, 8))),
        "down_weight": gaussian(seeds[4], (D, FF), 0.5, 3.0, ((0, 16), (1, 8))),
        "gate_a": gaussian(seeds[5], (STACKED, D), 1.0, 6.0, ((0, 128),)),
        "up_a": gaussian(seeds[6], (STACKED, D), 1.0, 6.0, ((0, 128),)),
        "down_a": gaussian(seeds[7], (STACKED, FF), 1.0, 6.0, ((0, 128),)),
        "gate_b": gaussian(seeds[8], (STACKED, FF), 1.0, 6.0, ((0, 128),)),
        "up_b": gaussian(seeds[9], (STACKED, FF), 1.0, 6.0, ((0, 128),)),
        "down_b": gaussian(seeds[10], (STACKED, D), 1.0, 6.0, ((0, 128),)),
    }


def merge_one(weight, factor_a, factor_b, row_scale):
    scaled = (row_scale[:, None] * factor_a.astype(jnp.float32)).astype(jnp.bfloat16)
    update = jnp.dot(factor_b.T, scaled, preferred_element_type=jnp.float32)
    return (weight.astype(jnp.float32) + update).astype(jnp.bfloat16)


def reference(sample_counts, slot_silo, gate_weight, up_weight, down_weight, gate_a, up_a, down_a, gate_b, up_b, down_b):
    counts_f = sample_counts.astype(jnp.float32)
    shares = counts_f / jnp.sum(counts_f)
    slot_ids = (jnp.arange(SILOS * RANK, dtype=jnp.int32) // RANK).astype(jnp.int32)
    silo_ids = slot_silo[slot_ids]
    row_scale = shares[silo_ids]
    merged_gate = merge_one(gate_weight, gate_a, gate_b, row_scale)
    merged_up = merge_one(up_weight, up_a, up_b, row_scale)
    merged_down = merge_one(down_weight, down_a, down_b, row_scale)
    return (merged_gate, merged_up, merged_down)
```

```python
import jax
import jax.numpy as jnp
from jax import lax
from jax.experimental import pallas as pl
from jax.experimental.pallas import tpu as pltpu
from jax.sharding import PartitionSpec as P

RANK = 16
MESH = pl.DeviceIdType.MESH
UNIT = 512
MB = 256


def kernel(
    counts_ref, slots_ref, gw, uw, dw, ga, ua, da, gb, ub, db,
    o0, o1, o2,
    abuf, bbuf, scaled, bt, scale,
    w_sem, a_send, a_recv, b_send, b_recv, z_send, z_recv, g_send, g_recv,
):
    ny, nx, nc, sub, _ = abuf.shape
    ranks = ny * nx * nc * sub
    row, col = lax.axis_index("row"), lax.axis_index("col")
    y, x = row // nx, lax.rem(row, nx)
    z, core = col // 2, lax.rem(col, 2)
    nz = nc // 2
    yp, ym = lax.rem(y + 1, ny), lax.rem(y + ny - 1, ny)
    xp, xm = lax.rem(x + 1, nx), lax.rem(x + nx - 1, nx)
    zp, zm, zo = (lax.rem(z + d, nz) for d in (1, nz - 1, 2))
    dev_xp, dev_xm = (y * nx + xp, col), (y * nx + xm, col)
    dev_yp, dev_ym = (yp * nx + x, col), (ym * nx + x, col)
    col_zp, col_zm, col_zo = zp * 2 + core, zm * 2 + core, zo * 2 + core
    dev_zp, dev_zm = (row, col_zp), (row, col_zm)
    mate = 1 - core
    dev_mate = (row, z * 2 + mate)

    barrier = pltpu.get_barrier_semaphore()
    col_peers = [lax.rem(col + k, nc) for k in range(1, nc)]
    row_peers = [
        lax.rem(y + dy, ny) * nx + lax.rem(x + dx, nx)
        for dy in range(ny)
        for dx in range(nx)
        if dy or dx
    ]
    for c in col_peers:
        pl.semaphore_signal(barrier, inc=1, device_id=(row, c), device_id_type=MESH)
    for r in row_peers:
        pl.semaphore_signal(barrier, inc=1, device_id=(r, col), device_id_type=MESH)
    pl.semaphore_wait(barrier, len(col_peers) + len(row_peers))

    started = []

    def send(src, dst, ssem, rsem, dev):
        copy = pltpu.make_async_remote_copy(
            src_ref=src, dst_ref=dst, send_sem=ssem, recv_sem=rsem,
            device_id=dev, device_id_type=MESH,
        )
        copy.start()
        started.append(copy)

    def arrived(ref, sem):
        pltpu.make_async_copy(ref, ref, sem).wait()

    a_parts = []
    at = 0
    for src in (ga, ua, da):
        n = src.shape[1] // nc
        a_parts.append((src, at, n))
        at += n
    b_parts = []
    at = 0
    for src in (gb, ub, db):
        n = src.shape[1] // (ny * nx)
        b_parts.append((src, at, n))
        at += n

    def spread_a(p):
        src, at, n = a_parts[p]
        for k, c in enumerate(col_peers):
            send(
                src.at[:, pl.ds(pl.multiple_of(c * n, n), n)],
                abuf.at[y, x, col, :, pl.ds(at, n)],
                a_send.at[p, k], a_recv.at[p], (row, c),
            )
        pltpu.make_async_copy(
            src.at[:, pl.ds(pl.multiple_of(col * n, n), n)],
            abuf.at[y, x, col, :, pl.ds(at, n)],
            a_recv.at[p],
        ).start()

    def spread_b(p):
        src, at, n = b_parts[p]
        for k, r in enumerate(row_peers):
            send(
                src.at[:, pl.ds(pl.multiple_of(r * n, n), n)],
                bbuf.at[y, x, col, :, pl.ds(at, n)],
                b_send.at[p, k], b_recv.at[p], (r, col),
            )
        pltpu.make_async_copy(
            src.at[:, pl.ds(pl.multiple_of(row * n, n), n)],
            bbuf.at[y, x, col, :, pl.ds(at, n)],
            b_recv.at[p],
        ).start()

    for p in range(3):
        spread_a(p)
        spread_b(p)
    outs = (o0, o1, o2)
    loads = [
        pltpu.make_async_copy(w, o, w_sem.at[i])
        for i, (w, o) in enumerate(zip((gw, uw, dw), outs))
    ]
    for load in loads:
        load.start()

    slots = slots_ref.shape[1]
    lane = lax.broadcasted_iota(jnp.int32, (ranks, slots), 1)
    slot = lax.broadcasted_iota(jnp.int32, (ranks, slots), 0) // RANK
    silo = jnp.sum(
        jnp.where(slot == lane, slots_ref[...].astype(jnp.float32), 0.0), axis=1, keepdims=True
    )
    counts = counts_ref[...].astype(jnp.float32)
    shares = counts / jnp.sum(counts, axis=1, keepdims=True)
    row_scale = jnp.sum(
        jnp.where(silo == lane.astype(jnp.float32), shares, 0.0), axis=1, keepdims=True
    )
    scale[...] = jnp.broadcast_to(row_scale, scale.shape)

    def b_block(p, ys, c):
        _, at, n = b_parts[p]
        return bbuf.at[ys, :, c, :, pl.ds(at, n)]

    whole, low, high = pl.ds(0, ny), pl.ds(0, ny // 2), pl.ds(ny // 2, ny // 2)

    def b_send_block(p, ys, c, k, dev):
        ref = b_block(p, ys, c)
        send(ref, ref, z_send.at[p, k], z_recv.at[p, k], dev)

    def zb1(p):
        arrived(b_block(p, whole, col), b_recv.at[p])
        b_send_block(p, whole, col, 0, dev_zp)
        b_send_block(p, whole, col, 1, dev_zm)
        b_send_block(p, whole, col, 4, dev_mate)

    def zb2(p):
        arrived(b_block(p, whole, col_zm), z_recv.at[p, 0])
        b_send_block(p, low, col_zm, 2, dev_zp)
        b_send_block(p, whole, col_zm, 5, dev_mate)
        arrived(b_block(p, whole, col_zp), z_recv.at[p, 1])
        b_send_block(p, high, col_zp, 3, dev_zm)
        b_send_block(p, whole, col_zp, 6, dev_mate)

    def zb3(p):
        arrived(b_block(p, low, col_zo), z_recv.at[p, 2])
        arrived(b_block(p, high, col_zo), z_recv.at[p, 3])
        b_send_block(p, whole, col_zo, 7, dev_mate)

    def b_done(p):
        for k, c in ((4, z), (5, zm), (6, zp), (7, zo)):
            arrived(b_block(p, whole, c * 2 + mate), z_recv.at[p, k])
        _, at, n = b_parts[p]

        def turn(m, carry):
            cols = pl.ds(pl.multiple_of(at + m * MB, MB), MB)
            bt[cols, :] = bbuf[:, :, :, :, cols].reshape(ranks, MB).T
            return carry

        lax.fori_loop(0, n // MB, turn, 0)

    half, quarter = nc // 2, nc // 4
    c_lo, c_hi = pl.ds(0, half), pl.ds(half, half)
    q0, q1, q2, q3 = (pl.ds(i * quarter, quarter) for i in range(4))
    every = pl.ds(0, nx)

    def a_ref(ys, xs, cs, u):
        return abuf.at[ys, xs, cs, :, pl.ds(u * UNIT, UNIT)]

    def move(u, d, ref, dev):
        send(ref, ref, g_send.at[u, d], g_recv.at[u, d], dev)

    def p1(u):
        for p, (_, at, n) in enumerate(a_parts):
            if at == u * UNIT:
                arrived(abuf.at[y, x, :, :, pl.ds(at, n)], a_recv.at[p])
        move(u, 0, a_ref(y, x, c_lo, u), dev_xp)
        move(u, 1, a_ref(y, x, c_lo, u), dev_xm)
        move(u, 2, a_ref(y, x, c_hi, u), dev_yp)
        move(u, 3, a_ref(y, x, c_hi, u), dev_ym)

    def r1(u):
        for d, ref, onward, dev in (
            (0, a_ref(y, xm, c_lo, u), a_ref(y, xm, q0, u), dev_xp),
            (1, a_ref(y, xp, c_lo, u), a_ref(y, xp, q1, u), dev_xm),
            (2, a_ref(ym, x, c_hi, u), a_ref(ym, x, q2, u), dev_yp),
            (3, a_ref(yp, x, c_hi, u), a_ref(yp, x, q3, u), dev_ym),
        ):
            arrived(ref, g_recv.at[u, d])
            move(u, 4 + d, onward, dev)

    xo, yo = lax.rem(x + 2, nx), lax.rem(y + 2, ny)

    def p2(u):
        arrived(a_ref(y, xo, q0, u), g_recv.at[u, 4])
        arrived(a_ref(y, xo, q1, u), g_recv.at[u, 5])
        move(u, 8, a_ref(y, every, c_lo, u), dev_yp)
        move(u, 9, a_ref(y, every, c_lo, u), dev_ym)
        arrived(a_ref(yo, x, q2, u), g_recv.at[u, 6])
        arrived(a_ref(yo, x, q3, u), g_recv.at[u, 7])
        move(u, 10, a_ref(whole, x, c_hi, u), dev_xp)
        move(u, 11, a_ref(whole, x, c_hi, u), dev_xm)

    def r2(u):
        for d, ref, onward, dev in (
            (8, a_ref(ym, every, c_lo, u), a_ref(ym, every, q0, u), dev_yp),
            (9, a_ref(yp, every, c_lo, u), a_ref(yp, every, q1, u), dev_ym),
            (10, a_ref(whole, xm, c_hi, u), a_ref(whole, xm, q2, u), dev_xp),
            (11, a_ref(whole, xp, c_hi, u), a_ref(whole, xp, q3, u), dev_xm),
        ):
            arrived(ref, g_recv.at[u, d])
            move(u, 4 + d, onward, dev)

    waited = set()

    def compute(u):
        arrived(a_ref(yo, every, q0, u), g_recv.at[u, 12])
        arrived(a_ref(yo, every, q1, u), g_recv.at[u, 13])
        arrived(a_ref(whole, xo, q2, u), g_recv.at[u, 14])
        arrived(a_ref(whole, xo, q3, u), g_recv.at[u, 15])
        p = max(i for i in range(3) if a_parts[i][1] <= u * UNIT)
        if p not in waited:
            waited.add(p)
            loads[p].wait()
        out = outs[p]
        ocols = pl.ds(u * UNIT - a_parts[p][1], UNIT)
        bat = b_parts[p][1]
        block = nc * sub

        def rescale(r, carry):
            rows = pl.ds(pl.multiple_of(r * block, block), block)
            a = abuf[r // nx, lax.rem(r, nx), :, :, pl.ds(u * UNIT, UNIT)]
            a = a.astype(jnp.float32).reshape(block, UNIT)
            s = scale[rows, :]
            s = jnp.concatenate([s] * (UNIT // s.shape[1]), axis=1)
            scaled[rows, :] = (a * s).astype(jnp.bfloat16)
            return carry

        lax.fori_loop(0, ny * nx, rescale, 0)

        def multiply(m, carry):
            orows = pl.ds(pl.multiple_of(m * MB, MB), MB)
            brows = pl.ds(pl.multiple_of(bat + m * MB, MB), MB)
            update = jnp.dot(bt[brows, :], scaled[...], preferred_element_type=jnp.float32)
            out[orows, ocols] = (out[orows, ocols].astype(jnp.float32) + update).astype(
                out.dtype
            )
            return carry

        lax.fori_loop(0, out.shape[0] // MB, multiply, 0)

    units = abuf.shape[4] // UNIT
    b_plan = {
        0: [(zb1, 0)],
        2: [(zb2, 0), (zb1, 1)],
        3: [(zb3, 0)],
        4: [(b_done, 0), (zb2, 1), (zb1, 2)],
        5: [(zb3, 1), (zb2, 2)],
        6: [(b_done, 1), (zb3, 2)],
        7: [(b_done, 2)],
    }
    c_plan = {5: [0], 6: [1], 7: [2], 8: [3, 4]}
    for u in range(5, units):
        c_plan[u + 4] = [u]
    for s in range(units + 4):
        for stage, lag in ((r2, 3), (p2, 2), (r1, 1), (p1, 0)):
            if 0 <= s - lag < units:
                stage(s - lag)
        for stage, p in b_plan.get(s, []):
            stage(p)
        for u in c_plan.get(s, []):
            compute(u)
    for copy in started:
        copy.wait_send()


def local(
    sample_counts, slot_silo, gate_weight, up_weight, down_weight,
    gate_a, up_a, down_a, gate_b, up_b, down_b,
):
    n_row, n_col = lax.axis_size("row"), lax.axis_size("col")
    ny = nx = 4
    sub = gate_a.shape[0]
    ranks = n_row * n_col * sub
    a_cols = sum(a.shape[1] // n_col for a in (gate_a, up_a, down_a))
    b_cols = sum(b.shape[1] // n_row for b in (gate_b, up_b, down_b))
    weights = (gate_weight, up_weight, down_weight)
    units = a_cols // UNIT
    dma = pltpu.SemaphoreType.DMA
    vmem = pl.BlockSpec(memory_space=pltpu.VMEM)
    hbm = pl.BlockSpec(memory_space=pltpu.HBM)
    return pl.pallas_call(
        kernel,
        out_shape=tuple(pltpu.VMEM(w.shape, w.dtype) for w in weights),
        in_specs=[vmem] * 2 + [hbm] * 9,
        out_specs=(vmem,) * 3,
        scratch_shapes=[
            pltpu.VMEM((ny, nx, n_col, sub, a_cols), jnp.bfloat16),
            pltpu.VMEM((ny, nx, n_col, sub, b_cols), jnp.bfloat16),
            pltpu.VMEM((ranks, UNIT), jnp.bfloat16),
            pltpu.VMEM((b_cols, ranks), jnp.bfloat16),
            pltpu.VMEM((ranks, 128), jnp.float32),
            dma((3,)),
            dma((3, n_col - 1)),
            dma((3,)),
            dma((3, n_row - 1)),
            dma((3,)),
            dma((3, 8)),
            dma((3, 8)),
            dma((units, 16)),
            dma((units, 16)),
        ],
        compiler_params=pltpu.CompilerParams(
            collective_id=0, has_side_effects=True, vmem_limit_bytes=50 * 1024 * 1024
        ),
    )(sample_counts.reshape(1, -1), slot_silo.reshape(1, -1), *weights,
      gate_a, up_a, down_a, gate_b, up_b, down_b)


def solution(mesh):
    spread, tile = P(("row", "col"), None), P("row", "col")
    return jax.shard_map(
        local,
        mesh=mesh,
        in_specs=(P(), P(), tile, tile, tile, spread, spread, spread, spread, spread, spread),
        out_specs=(tile, tile, tile),
        check_vma=False,
    )
```

```python
import jax
import jax.numpy as jnp
from jax import lax
from jax.experimental import pallas as pl
from jax.experimental.pallas import tpu as pltpu
from jax.sharding import PartitionSpec as P

RANK = 16
MESH = pl.DeviceIdType.MESH
UNIT = 256
WIDE = 512
TALL = 896
LAG = (0, 2, 4, 6, 8)
WINDOW = 8


def kernel(
    counts_hbm, slots_hbm, gw, uw, dw, ga, ua, da, gb, ub, db,
    o0, o1, o2,
    abuf, bbuf, scaled, scale, counts_ref, slots_ref,
    s_sem, w_sem, sent, a_recv, b_recv, z_recv, g_recv,
):
    ny, nx, nc, sub, _ = abuf.shape
    ranks = ny * nx * nc * sub
    row, col = lax.axis_index("row"), lax.axis_index("col")
    y, x = row // nx, lax.rem(row, nx)
    z, core = col // 2, lax.rem(col, 2)
    nz = nc // 2
    yp, ym = lax.rem(y + 1, ny), lax.rem(y + ny - 1, ny)
    xp, xm = lax.rem(x + 1, nx), lax.rem(x + nx - 1, nx)
    zp, zm, zo = (lax.rem(z + d, nz) for d in (1, nz - 1, 2))
    dev_xp, dev_xm = (y * nx + xp, col), (y * nx + xm, col)
    dev_yp, dev_ym = (yp * nx + x, col), (ym * nx + x, col)
    col_zp, col_zm, col_zo = zp * 2 + core, zm * 2 + core, zo * 2 + core
    dev_zp, dev_zm = (row, col_zp), (row, col_zm)
    mate = 1 - core
    dev_mate = (row, z * 2 + mate)

    small = [
        pltpu.make_async_copy(h, v, s_sem.at[i])
        for i, (h, v) in enumerate(((counts_hbm, counts_ref), (slots_hbm, slots_ref)))
    ]
    for copy in small:
        copy.start()
    barrier = pltpu.get_barrier_semaphore()
    col_peers = [lax.rem(col + k, nc) for k in range(1, nc)]
    row_peers = [
        lax.rem(y + dy, ny) * nx + lax.rem(x + dx, nx)
        for dy in range(ny)
        for dx in range(nx)
        if dy or dx
    ]
    for c in col_peers:
        pl.semaphore_signal(barrier, inc=1, device_id=(row, c), device_id_type=MESH)
    for r in row_peers:
        pl.semaphore_signal(barrier, inc=1, device_id=(r, col), device_id_type=MESH)
    pl.semaphore_wait(barrier, len(col_peers) + len(row_peers))

    def send(src, dst, kind, rsem, dev):
        pltpu.make_async_remote_copy(
            src_ref=src, dst_ref=dst, send_sem=sent.at[kind], recv_sem=rsem,
            device_id=dev, device_id_type=MESH,
        ).start()

    def arrived(ref, sem):
        pltpu.make_async_copy(ref, ref, sem).wait()

    a_parts = []
    at = 0
    for src in (ga, ua, da):
        n = src.shape[1] // nc
        a_parts.append((src, at, n))
        at += n
    b_parts, b_start = [], []
    at = 0
    for src in (gb, ub, db):
        total = src.shape[1] // (ny * nx)
        b_start.append(at)
        n = min(total, TALL)
        for begin in range(0, total, n):
            b_parts.append((src, total, begin, at + begin, n))
        at += total

    def spread_a(p):
        src, at, n = a_parts[p]
        for c in col_peers:
            send(
                src.at[:, pl.ds(pl.multiple_of(c * n, n), n)],
                abuf.at[y, x, col, :, pl.ds(at, n)],
                0, a_recv.at[p], (row, c),
            )
        pltpu.make_async_copy(
            src.at[:, pl.ds(pl.multiple_of(col * n, n), n)],
            abuf.at[y, x, col, :, pl.ds(at, n)],
            a_recv.at[p],
        ).start()

    def spread_b(p):
        src, total, begin, at, n = b_parts[p]
        for r in row_peers:
            send(
                src.at[:, pl.ds(pl.multiple_of(r * total + begin, 128), n)],
                bbuf.at[y, x, col, :, pl.ds(at, n)],
                1, b_recv.at[p], (r, col),
            )
        pltpu.make_async_copy(
            src.at[:, pl.ds(pl.multiple_of(row * total + begin, 128), n)],
            bbuf.at[y, x, col, :, pl.ds(at, n)],
            b_recv.at[p],
        ).start()

    for p in range(3):
        spread_a(p)
        if p < 2:
            spread_b(p)
    outs = (o0, o1, o2)
    loads = [
        pltpu.make_async_copy(w, o, w_sem.at[i])
        for i, (w, o) in enumerate(zip((gw, uw, dw), outs))
    ]
    for load in loads:
        load.start()

    for copy in small:
        copy.wait()
    slots = slots_ref.shape[1]
    lane = lax.broadcasted_iota(jnp.int32, (ranks, slots), 1)
    slot = lax.broadcasted_iota(jnp.int32, (ranks, slots), 0) // RANK
    silo = jnp.sum(
        jnp.where(slot == lane, slots_ref[...].astype(jnp.float32), 0.0), axis=1, keepdims=True
    )
    counts = counts_ref[...].astype(jnp.float32)
    shares = counts / jnp.sum(counts, axis=1, keepdims=True)
    row_scale = jnp.sum(
        jnp.where(silo == lane.astype(jnp.float32), shares, 0.0), axis=1, keepdims=True
    )
    scale[...] = jnp.broadcast_to(row_scale, scale.shape)

    def b_block(p, ys, c):
        _, _, _, at, n = b_parts[p]
        return bbuf.at[ys, :, c, :, pl.ds(at, n)]

    whole, low, high = pl.ds(0, ny), pl.ds(0, ny // 2), pl.ds(ny // 2, ny // 2)

    def b_send_block(p, ys, c, k, dev):
        ref = b_block(p, ys, c)
        send(ref, ref, 2, z_recv.at[p, k], dev)

    def zb1(p):
        arrived(b_block(p, whole, col), b_recv.at[p])
        b_send_block(p, whole, col, 0, dev_zp)
        b_send_block(p, whole, col, 1, dev_zm)
        b_send_block(p, whole, col, 3, dev_mate)

    def zb2(p):
        arrived(b_block(p, whole, col_zm), z_recv.at[p, 0])
        b_send_block(p, low, col_zm, 2, dev_zp)
        b_send_block(p, whole, col_zm, 3, dev_mate)
        arrived(b_block(p, whole, col_zp), z_recv.at[p, 1])
        b_send_block(p, high, col_zp, 2, dev_zm)
        b_send_block(p, whole, col_zp, 3, dev_mate)

    def zb3(p):
        arrived(b_block(p, whole, col_zo), z_recv.at[p, 2])
        b_send_block(p, whole, col_zo, 3, dev_mate)

    def b_done(p):
        _, _, _, at, n = b_parts[p]
        arrived(bbuf.at[:, :, pl.ds(0, nz), :, pl.ds(at, n)], z_recv.at[p, 3])

    half, quarter = nc // 2, nc // 4
    c_lo, c_hi = pl.ds(0, half), pl.ds(half, half)
    q0, q1, q2, q3 = (pl.ds(i * quarter, quarter) for i in range(4))
    every = pl.ds(0, nx)

    def a_ref(ys, xs, cs, u):
        return abuf.at[ys, xs, cs, :, pl.ds(u * UNIT, UNIT)]

    def move(u, d, ref, dev):
        send(ref, ref, 3, g_recv.at[u % WINDOW, d], dev)

    def p1(u):
        for p, (_, at, n) in enumerate(a_parts):
            if at == u * UNIT:
                arrived(abuf.at[y, x, :, :, pl.ds(at, n)], a_recv.at[p])
        move(u, 0, a_ref(y, x, c_lo, u), dev_xp)
        move(u, 1, a_ref(y, x, c_lo, u), dev_xm)
        move(u, 2, a_ref(y, x, c_hi, u), dev_yp)
        move(u, 3, a_ref(y, x, c_hi, u), dev_ym)

    def r1(u):
        for d, ref, onward, dev in (
            (0, a_ref(y, xm, c_lo, u), a_ref(y, xm, q0, u), dev_xp),
            (1, a_ref(y, xp, c_lo, u), a_ref(y, xp, q1, u), dev_xm),
            (2, a_ref(ym, x, c_hi, u), a_ref(ym, x, q2, u), dev_yp),
            (3, a_ref(yp, x, c_hi, u), a_ref(yp, x, q3, u), dev_ym),
        ):
            arrived(ref, g_recv.at[u % WINDOW, d])
            move(u, 4, onward, dev)

    def p2(u):
        arrived(a_ref(y, x, pl.ds(0, nc), u), g_recv.at[u % WINDOW, 4])
        move(u, 5, a_ref(y, every, c_lo, u), dev_yp)
        move(u, 6, a_ref(y, every, c_lo, u), dev_ym)
        move(u, 7, a_ref(whole, x, c_hi, u), dev_xp)
        move(u, 8, a_ref(whole, x, c_hi, u), dev_xm)

    def r2(u):
        for d, ref, onward, dev in (
            (5, a_ref(ym, every, c_lo, u), a_ref(ym, every, q0, u), dev_yp),
            (6, a_ref(yp, every, c_lo, u), a_ref(yp, every, q1, u), dev_ym),
            (7, a_ref(whole, xm, c_hi, u), a_ref(whole, xm, q2, u), dev_xp),
            (8, a_ref(whole, xp, c_hi, u), a_ref(whole, xp, q3, u), dev_xm),
        ):
            arrived(ref, g_recv.at[u % WINDOW, d])
            move(u, 9, onward, dev)

    flat = bbuf.reshape(ranks, bbuf.shape[4])
    block = nc * sub
    waited = set()

    def complete(u):
        arrived(a_ref(y, every, pl.ds(0, nc), u), g_recv.at[u % WINDOW, 9])

    def compute(us, m):
        begin, n = us[0] * UNIT, len(us) * UNIT
        p = part_of(us[0])
        if p not in waited:
            waited.add(p)
            loads[p].wait()
        out = outs[p]
        ocols = pl.ds(begin - a_parts[p][1], n)

        def rescale(r, carry):
            rows = pl.ds(pl.multiple_of(r * block, block), block)
            a = abuf[r // nx, lax.rem(r, nx), :, :, pl.ds(begin, n)]
            a = a.astype(jnp.float32).reshape(block, n)
            s = scale[rows, :]
            s = jnp.concatenate([s] * (n // s.shape[1]), axis=1)
            scaled[rows, pl.ds(0, n)] = (a * s).astype(jnp.bfloat16)
            return carry

        if m == 0:
            lax.fori_loop(0, ny * nx, rescale, 0)
        tall = min(out.shape[0], TALL)
        orows = pl.ds(m * tall, tall)
        update = lax.dot_general(
            flat[:, pl.ds(b_start[p] + m * tall, tall)],
            scaled[:, pl.ds(0, n)],
            (((0,), (0,)), ((), ())),
            preferred_element_type=jnp.float32,
        )
        out[orows, ocols] = (out[orows, ocols].astype(jnp.float32) + update).astype(
            out.dtype
        )

    def part_of(u):
        return max(i for i in range(3) if a_parts[i][1] <= u * UNIT)

    units = abuf.shape[4] // UNIT
    b_plan = {
        0: [(zb1, 0), (spread_b, 2)],
        1: [(zb1, 1), (spread_b, 3)],
        2: [(spread_b, 4)],
        4: [(zb2, 0), (zb1, 2)],
        7: [(zb3, 0), (zb2, 1), (zb1, 3)],
        10: [(zb3, 1), (zb2, 2), (zb1, 4)],
        11: [(b_done, 0), (b_done, 1)],
        13: [(zb3, 2), (zb2, 3)],
        15: [(zb3, 3), (zb2, 4)],
        17: [(zb3, 4), (b_done, 2), (b_done, 3)],
        18: [(b_done, 4)],
    }
    ready = {0: 12, 1: 17, 2: 19}
    wide = WIDE // UNIT
    work = []
    for u in range(0, units, wide):
        p = part_of(u)
        tiles = max(1, outs[p].shape[0] // TALL)
        if u + wide < units:
            work += [(list(range(u, u + wide)), m, ready[p]) for m in range(tiles)]
        else:
            work += [([v], m, 0) for v in range(u, units) for m in range(tiles)]
    c_plan, step = {}, 0
    for us, m, least in work:
        step = max(step + 1, us[-1] + LAG[4], least)
        c_plan.setdefault(min(step, units - 1 + LAG[4]), []).append((us, m))
    for s in range(units + LAG[4]):
        for stage, lag in (
            (r2, LAG[3]), (p2, LAG[2]), (r1, LAG[1]), (p1, LAG[0]), (complete, LAG[4])
        ):
            if 0 <= s - lag < units:
                stage(s - lag)
        for stage, p in b_plan.get(s, []):
            stage(p)
        for us, m in c_plan.get(s, []):
            compute(us, m)
    af = abuf.reshape(ny * nx * nc, sub, abuf.shape[4])
    bf = bbuf.reshape(ny * nx * nc, sub, bbuf.shape[4])
    a_count, b_count = ny * nx * nc, ny * nx
    arrived(af.at[pl.ds(0, nc - 1)], sent.at[0])
    arrived(bf.at[pl.ds(0, b_count - 1)], sent.at[1])
    arrived(bf.at[pl.ds(0, 7 * b_count)], sent.at[2])
    arrived(af.at[pl.ds(0, a_count - nc)], sent.at[3])


def local(
    sample_counts, slot_silo, gate_weight, up_weight, down_weight,
    gate_a, up_a, down_a, gate_b, up_b, down_b,
):
    n_row, n_col = lax.axis_size("row"), lax.axis_size("col")
    ny = nx = 4
    sub = gate_a.shape[0]
    ranks = n_row * n_col * sub
    a_cols = sum(a.shape[1] // n_col for a in (gate_a, up_a, down_a))
    b_cols = sum(b.shape[1] // n_row for b in (gate_b, up_b, down_b))
    weights = (gate_weight, up_weight, down_weight)
    pieces = sum(
        max(1, b.shape[1] // n_row // TALL) for b in (gate_b, up_b, down_b)
    )
    dma = pltpu.SemaphoreType.DMA
    vmem = pl.BlockSpec(memory_space=pltpu.VMEM)
    hbm = pl.BlockSpec(memory_space=pltpu.HBM)
    return pl.pallas_call(
        kernel,
        out_shape=tuple(pltpu.VMEM(w.shape, w.dtype) for w in weights),
        in_specs=[hbm] * 11,
        out_specs=(vmem,) * 3,
        scratch_shapes=[
            pltpu.VMEM((ny, nx, n_col, sub, a_cols), jnp.bfloat16),
            pltpu.VMEM((ny, nx, n_col, sub, b_cols), jnp.bfloat16),
            pltpu.VMEM((ranks, WIDE), jnp.bfloat16),
            pltpu.VMEM((ranks, 128), jnp.float32),
            pltpu.VMEM((1, sample_counts.shape[0]), jnp.int32),
            pltpu.VMEM((1, slot_silo.shape[0]), jnp.int32),
            dma((2,)),
            dma((3,)),
            dma((4,)),
            dma((3,)),
            dma((pieces,)),
            dma((pieces, 4)),
            dma((WINDOW, 10)),
        ],
        compiler_params=pltpu.CompilerParams(
            collective_id=0, has_side_effects=True, vmem_limit_bytes=50 * 1024 * 1024
        ),
    )(sample_counts.reshape(1, -1), slot_silo.reshape(1, -1), *weights,
      gate_a, up_a, down_a, gate_b, up_b, down_b)


def solution(mesh):
    spread, tile = P(("row", "col"), None), P("row", "col")
    return jax.shard_map(
        local,
        mesh=mesh,
        in_specs=(P(), P(), tile, tile, tile, spread, spread, spread, spread, spread, spread),
        out_specs=(tile, tile, tile),
        check_vma=False,
    )
```

```python
import jax
import jax.numpy as jnp
from jax import lax
from jax.experimental import pallas as pl
from jax.experimental.pallas import tpu as pltpu
from jax.sharding import PartitionSpec as P

RANK = 16
MESH = pl.DeviceIdType.MESH
UNIT = 256
WIDE = 512
TALL = 896
LAG = (0, 2, 4, 5, 7)
AHEAD = 90
WINDOW = 10
PARTS = 4


def kernel(
    counts_hbm, slots_hbm, gw, uw, dw, ga, ua, da, gb, ub, db,
    o0, o1, o2,
    abuf, bbuf, scaled, scale, counts_ref, slots_ref,
    s_sem, w_sem, sent, a_recv, b_recv, z_recv, g_recv,
):
    ny, nx, nc, sub, _ = abuf.shape
    ranks = ny * nx * nc * sub
    row, col = lax.axis_index("row"), lax.axis_index("col")
    y, x = row // nx, lax.rem(row, nx)
    z, core = col // 2, lax.rem(col, 2)
    nz = nc // 2
    yp, ym = lax.rem(y + 1, ny), lax.rem(y + ny - 1, ny)
    xp, xm = lax.rem(x + 1, nx), lax.rem(x + nx - 1, nx)
    zp, zm, zo = (lax.rem(z + d, nz) for d in (1, nz - 1, 2))
    dev_xp, dev_xm = (y * nx + xp, col), (y * nx + xm, col)
    dev_yp, dev_ym = (yp * nx + x, col), (ym * nx + x, col)
    col_zp, col_zm, col_zo = zp * 2 + core, zm * 2 + core, zo * 2 + core
    dev_zp, dev_zm = (row, col_zp), (row, col_zm)
    mate = 1 - core
    dev_mate = (row, z * 2 + mate)

    small = [
        pltpu.make_async_copy(h, v, s_sem.at[i])
        for i, (h, v) in enumerate(((counts_hbm, counts_ref), (slots_hbm, slots_ref)))
    ]
    for copy in small:
        copy.start()
    barrier = pltpu.get_barrier_semaphore()
    col_peers = [lax.rem(col + k, nc) for k in range(1, nc)]
    row_peers = [
        lax.rem(y + dy, ny) * nx + lax.rem(x + dx, nx)
        for dy, dx in (
            (2, 2), (0, 1), (1, 0), (0, 3), (3, 0), (1, 2), (2, 1), (3, 2), (2, 3), (1, 1), (3, 3), (1, 3), (3, 1), (0, 2), (2, 0)
        )
    ]
    for c in col_peers:
        pl.semaphore_signal(barrier, inc=1, device_id=(row, c), device_id_type=MESH)
    for r in row_peers:
        pl.semaphore_signal(barrier, inc=1, device_id=(r, col), device_id_type=MESH)
    pl.semaphore_wait(barrier, len(col_peers) + len(row_peers))

    def send(src, dst, kind, rsem, dev):
        pltpu.make_async_remote_copy(
            src_ref=src, dst_ref=dst, send_sem=sent.at[kind], recv_sem=rsem,
            device_id=dev, device_id_type=MESH,
        ).start()

    def arrived(ref, sem):
        pltpu.make_async_copy(ref, ref, sem).wait()

    a_parts = []
    at = 0
    for src in (ga, ua, da):
        n = src.shape[1] // nc
        a_parts.append((src, at, n))
        at += n
    b_parts, b_start = [], []
    at = 0
    for src in (gb, ub, db):
        total = src.shape[1] // (ny * nx)
        b_start.append(at)
        n = min(total, TALL)
        for begin in range(0, total, n):
            b_parts.append((src, total, begin, at + begin, n))
        at += total

    a_pieces = []
    for src, at, n in a_parts:
        cuts = [0, UNIT, n] if at == 0 else [0, n]
        a_pieces += [(src, n, b, at + b, e - b) for b, e in zip(cuts, cuts[1:])]

    def spread_a(p):
        src, total, begin, at, n = a_pieces[p]
        for c in col_peers:
            send(
                src.at[:, pl.ds(pl.multiple_of(c * total + begin, 128), n)],
                abuf.at[y, x, col, :, pl.ds(at, n)],
                0, a_recv.at[p], (row, c),
            )
        pltpu.make_async_copy(
            src.at[:, pl.ds(pl.multiple_of(col * total + begin, 128), n)],
            abuf.at[y, x, col, :, pl.ds(at, n)],
            a_recv.at[p],
        ).start()

    def spread_b(p):
        src, total, begin, at, n = b_parts[p]
        for r in row_peers:
            send(
                src.at[:, pl.ds(pl.multiple_of(r * total + begin, 128), n)],
                bbuf.at[y, x, col, :, pl.ds(at, n)],
                1, b_recv.at[p], (r, col),
            )
        pltpu.make_async_copy(
            src.at[:, pl.ds(pl.multiple_of(row * total + begin, 128), n)],
            bbuf.at[y, x, col, :, pl.ds(at, n)],
            b_recv.at[p],
        ).start()

    for p in range(len(a_pieces)):
        spread_a(p)
        if p < 2:
            spread_b(p)
    outs = (o0, o1, o2)
    loads = [
        pltpu.make_async_copy(w, o, w_sem.at[i])
        for i, (w, o) in enumerate(zip((gw, uw, dw), outs))
    ]
    for load in loads:
        load.start()

    for copy in small:
        copy.wait()
    slots = slots_ref.shape[1]
    lane = lax.broadcasted_iota(jnp.int32, (ranks, slots), 1)
    slot = lax.broadcasted_iota(jnp.int32, (ranks, slots), 0) // RANK
    silo = jnp.sum(
        jnp.where(slot == lane, slots_ref[...].astype(jnp.float32), 0.0), axis=1, keepdims=True
    )
    counts = counts_ref[...].astype(jnp.float32)
    shares = counts / jnp.sum(counts, axis=1, keepdims=True)
    row_scale = jnp.sum(
        jnp.where(silo == lane.astype(jnp.float32), shares, 0.0), axis=1, keepdims=True
    )
    scale[...] = jnp.broadcast_to(row_scale, scale.shape)

    def b_block(p, ys, c):
        _, _, _, at, n = b_parts[p]
        return bbuf.at[ys, :, c, :, pl.ds(at, n)]

    whole, low, high = pl.ds(0, ny), pl.ds(0, ny // 2), pl.ds(ny // 2, ny // 2)

    def b_send_block(p, ys, c, k, dev):
        ref = b_block(p, ys, c)
        send(ref, ref, 2, z_recv.at[p, k], dev)

    def zb1(p):
        arrived(b_block(p, whole, col), b_recv.at[p])
        b_send_block(p, whole, col, 0, dev_zp)
        b_send_block(p, whole, col, 1, dev_zm)
        b_send_block(p, whole, col, 3, dev_mate)

    def zb2(p):
        arrived(b_block(p, whole, col_zm), z_recv.at[p, 0])
        b_send_block(p, low, col_zm, 2, dev_zp)
        b_send_block(p, whole, col_zm, 3, dev_mate)
        arrived(b_block(p, whole, col_zp), z_recv.at[p, 1])
        b_send_block(p, high, col_zp, 2, dev_zm)
        b_send_block(p, whole, col_zp, 3, dev_mate)

    def zb3(p):
        arrived(b_block(p, whole, col_zo), z_recv.at[p, 2])
        b_send_block(p, whole, col_zo, 3, dev_mate)

    def b_done(p):
        _, _, _, at, n = b_parts[p]
        arrived(bbuf.at[:, :, pl.ds(0, nz), :, pl.ds(at, n)], z_recv.at[p, 3])

    half, quarter = nc // 2, nc // 4
    c_lo, c_hi = pl.ds(0, half), pl.ds(half, half)
    q0, q1, q2, q3 = (pl.ds(i * quarter, quarter) for i in range(4))
    every = pl.ds(0, nx)

    def a_ref(ys, xs, cs, u):
        return abuf.at[ys, xs, cs, :, pl.ds(u * UNIT, UNIT)]

    def move(u, d, ref, dev):
        send(ref, ref, 3, g_recv.at[u % WINDOW, d], dev)

    def p1(u):
        for p, (_, _, _, at, n) in enumerate(a_pieces):
            if at == u * UNIT:
                arrived(abuf.at[y, x, :, :, pl.ds(at, n)], a_recv.at[p])
        move(u, 0, a_ref(y, x, c_lo, u), dev_xp)
        move(u, 1, a_ref(y, x, c_lo, u), dev_xm)
        move(u, 2, a_ref(y, x, c_hi, u), dev_yp)
        move(u, 3, a_ref(y, x, c_hi, u), dev_ym)

    def r1(u):
        for d, ref, onward, dev in (
            (0, a_ref(y, xm, c_lo, u), a_ref(y, xm, q0, u), dev_xp),
            (1, a_ref(y, xp, c_lo, u), a_ref(y, xp, q1, u), dev_xm),
            (2, a_ref(ym, x, c_hi, u), a_ref(ym, x, q2, u), dev_yp),
            (3, a_ref(yp, x, c_hi, u), a_ref(yp, x, q3, u), dev_ym),
        ):
            arrived(ref, g_recv.at[u % WINDOW, d])
            move(u, 4, onward, dev)

    def p2(u):
        arrived(a_ref(y, x, pl.ds(0, nc), u), g_recv.at[u % WINDOW, 4])
        move(u, 5, a_ref(y, every, c_lo, u), dev_yp)
        move(u, 6, a_ref(y, every, c_lo, u), dev_ym)
        move(u, 7, a_ref(whole, x, c_hi, u), dev_xp)
        move(u, 8, a_ref(whole, x, c_hi, u), dev_xm)

    def r2(u):
        for d, ref, onward, dev in (
            (5, a_ref(ym, every, c_lo, u), a_ref(ym, every, q0, u), dev_yp),
            (6, a_ref(yp, every, c_lo, u), a_ref(yp, every, q1, u), dev_ym),
            (7, a_ref(whole, xm, c_hi, u), a_ref(whole, xm, q2, u), dev_xp),
            (8, a_ref(whole, xp, c_hi, u), a_ref(whole, xp, q3, u), dev_xm),
        ):
            arrived(ref, g_recv.at[u % WINDOW, d])
            move(u, 9, onward, dev)

    flat = bbuf.reshape(ranks, bbuf.shape[4])
    block = nc * sub
    waited = set()

    def complete(u):
        arrived(a_ref(y, every, pl.ds(0, nc), u), g_recv.at[u % WINDOW, 9])

    def compute(us, m):
        begin, n = us[0] * UNIT, len(us) * UNIT
        p = part_of(us[0])
        if p not in waited:
            waited.add(p)
            loads[p].wait()
        out = outs[p]
        ocols = pl.ds(begin - a_parts[p][1], n)

        def rescale(r, carry):
            rows = pl.ds(pl.multiple_of(r * block, block), block)
            a = abuf[r // nx, lax.rem(r, nx), :, :, pl.ds(begin, n)]
            a = a.astype(jnp.float32).reshape(block, n)
            s = scale[rows, :]
            s = jnp.concatenate([s] * (n // s.shape[1]), axis=1)
            scaled[rows, pl.ds(0, n)] = (a * s).astype(jnp.bfloat16)
            return carry

        if m == 0:
            lax.fori_loop(0, ny * nx, rescale, 0)
        tall = min(out.shape[0], TALL)
        orows = pl.ds(m * tall, tall)
        update = lax.dot_general(
            flat[:, pl.ds(b_start[p] + m * tall, tall)],
            scaled[:, pl.ds(0, n)],
            (((0,), (0,)), ((), ())),
            preferred_element_type=jnp.float32,
        )
        out[orows, ocols] = (out[orows, ocols].astype(jnp.float32) + update).astype(
            out.dtype
        )

    def part_of(u):
        return max(i for i in range(3) if a_parts[i][1] <= u * UNIT)

    units = abuf.shape[4] // UNIT
    b_plan = {
        0: [(zb1, 0), (spread_b, 2)],
        1: [(zb1, 1), (spread_b, 3)],
        2: [(spread_b, 4)],
        4: [(zb2, 0), (zb1, 2)],
        7: [(zb3, 0), (zb2, 1), (zb1, 3)],
        10: [(zb3, 1), (zb2, 2), (zb1, 4)],
        11: [(b_done, 0), (b_done, 1)],
        13: [(zb3, 2), (zb2, 3)],
        15: [(zb3, 3), (zb2, 4)],
        17: [(zb3, 4), (b_done, 2), (b_done, 3)],
        18: [(b_done, 4)],
    }
    ready = {0: 12, 1: 17, 2: 19}
    wide = WIDE // UNIT
    work = []
    for u in range(0, units, wide):
        p = part_of(u)
        tiles = max(1, outs[p].shape[0] // TALL)
        if u + wide < units:
            work += [(list(range(u, u + wide)), m, ready[p]) for m in range(tiles)]
        else:
            work += [([v], m, 0) for v in range(u, units) for m in range(tiles)]
    c_plan, step = {}, 0
    for us, m, least in work:
        step = max(step + 1, 2 * (us[-1] + LAG[4]), 2 * least)
        c_plan.setdefault(min(step // 2, units - 1 + LAG[4]), []).append((us, m))
    order = (
        (p2, lambda u: u * AHEAD // 100 + LAG[2]),
        (r1, lambda u: u * AHEAD // 100 + LAG[1]),
        (p1, lambda u: u * AHEAD // 100 + LAG[0]),
        (r2, lambda u: u + LAG[3]),
        (complete, lambda u: u + LAG[4]),
    )
    for s in range(units + LAG[4]):
        for stage, when in order:
            for u in range(units):
                if when(u) == s:
                    stage(u)
        for stage, p in b_plan.get(s, []):
            stage(p)
        for us, m in c_plan.get(s, []):
            compute(us, m)
    af = abuf.reshape(ny * nx * nc, sub, abuf.shape[4])
    bf = bbuf.reshape(ny * nx * nc, sub, bbuf.shape[4])
    a_count, b_count = ny * nx * nc, ny * nx
    arrived(af.at[pl.ds(0, nc - 1)], sent.at[0])
    arrived(bf.at[pl.ds(0, b_count - 1)], sent.at[1])
    arrived(bf.at[pl.ds(0, 7 * b_count)], sent.at[2])
    arrived(af.at[pl.ds(0, a_count - nc)], sent.at[3])


def write_out(i0, i1, i2, o0, o1, o2, sem):
    copies = []
    for k, (i, o) in enumerate(((i0, o0), (i1, o1), (i2, o2))):
        n = i.shape[0] // PARTS
        for m in range(PARTS):
            rows = pl.ds(m * n, n)
            copies.append(pltpu.make_async_copy(i.at[rows], o.at[rows], sem.at[k, m]))
    for copy in copies:
        copy.start()
    for copy in copies:
        copy.wait()


def local(
    sample_counts, slot_silo, gate_weight, up_weight, down_weight,
    gate_a, up_a, down_a, gate_b, up_b, down_b,
):
    n_row, n_col = lax.axis_size("row"), lax.axis_size("col")
    ny = nx = 4
    sub = gate_a.shape[0]
    ranks = n_row * n_col * sub
    a_cols = sum(a.shape[1] // n_col for a in (gate_a, up_a, down_a))
    b_cols = sum(b.shape[1] // n_row for b in (gate_b, up_b, down_b))
    weights = (gate_weight, up_weight, down_weight)
    pieces = sum(
        max(1, b.shape[1] // n_row // TALL) for b in (gate_b, up_b, down_b)
    )
    dma = pltpu.SemaphoreType.DMA
    vmem = pl.BlockSpec(memory_space=pltpu.VMEM)
    hbm = pl.BlockSpec(memory_space=pltpu.HBM)
    results = pl.pallas_call(
        kernel,
        out_shape=tuple(pltpu.VMEM(w.shape, w.dtype) for w in weights),
        in_specs=[hbm] * 11,
        out_specs=(vmem,) * 3,
        scratch_shapes=[
            pltpu.VMEM((ny, nx, n_col, sub, a_cols), jnp.bfloat16),
            pltpu.VMEM((ny, nx, n_col, sub, b_cols), jnp.bfloat16),
            pltpu.VMEM((ranks, WIDE), jnp.bfloat16),
            pltpu.VMEM((ranks, 128), jnp.float32),
            pltpu.VMEM((1, sample_counts.shape[0]), jnp.int32),
            pltpu.VMEM((1, slot_silo.shape[0]), jnp.int32),
            dma((2,)),
            dma((3,)),
            dma((4,)),
            dma((4,)),
            dma((pieces,)),
            dma((pieces, 4)),
            dma((WINDOW, 10)),
        ],
        compiler_params=pltpu.CompilerParams(
            collective_id=0, has_side_effects=True, vmem_limit_bytes=50 * 1024 * 1024
        ),
    )(sample_counts.reshape(1, -1), slot_silo.reshape(1, -1), *weights,
      gate_a, up_a, down_a, gate_b, up_b, down_b)
    anywhere = pl.BlockSpec(memory_space=pl.ANY)
    return pl.pallas_call(
        write_out,
        out_shape=tuple(jax.ShapeDtypeStruct(w.shape, w.dtype) for w in weights),
        in_specs=[anywhere] * 3,
        out_specs=(hbm,) * 3,
        scratch_shapes=[dma((3, PARTS))],
        compiler_params=pltpu.CompilerParams(vmem_limit_bytes=2 * 1024 * 1024),
    )(*results)


def solution(mesh):
    spread, tile = P(("row", "col"), None), P("row", "col")
    return jax.shard_map(
        local,
        mesh=mesh,
        in_specs=(P(), P(), tile, tile, tile, spread, spread, spread, spread, spread, spread),
        out_specs=(tile, tile, tile),
        check_vma=False,
    )
```
